32 devices in a mesh: epoch: 4 (over z), vel: 8 (over y, x, core).
Axes of the slice: x: 2, y: 2, z: 4, core: 2. Of those that a mesh axis runs over, the one named last changes fastest.
Arguments:
- science: float32 [8, 32, 1024], P('epoch', 'vel'), may hold values from -6 to 6
- variance: float32 [8, 32, 1024], P('epoch', 'vel'), may hold values from 0.25 to 4
- psf: float32 [8, 9], P('epoch'), may hold values from 0.05 to 1
- shifts: int32 [2, 8, 8], P(None, None, 'vel'), may hold values from -16 to 16, as said below
Outputs:
- likelihood: float32 [8, 32, 1024], P('vel', 'epoch')
The draws below stay inside these ranges and needn't reach their ends.
Inputs may be any that keep to these rules, and one draw needn't show every extreme that they name: For each velocity, the shifts of epoch e are the floor of the velocity's integer rates times the epoch's time over the span of the times; the first epoch's shifts are zero, and times rise with the epoch.
All inputs are finite; a program needn't handle non-finite values.
Results may differ from the reference program's by a relative error of at most 0.0003.
Values sent between devices are 32-bit elements; how exact they have to be, the bound alone decides.
No kernel may reach another device: no remote copies, remote signals or barrier semaphores. Data moves between devices by JAX's collectives and lax.ppermute only.
A program may use at most 64 MiB of HBM per device.

```python
import math
import jax
import jax.numpy as jnp
from jax import lax

EPOCHS = 8
TAPS = 9
MAXS = 16
W = 1024
H = 32
V = 8


def draw_shifts(key, part):
    key_col = jax.random.fold_in(key, 11)
    key_row = jax.random.fold_in(key, 23)
    key_time = jax.random.fold_in(key, 37)
    rate_col = jax.random.randint(key_col, (V,), -MAXS, MAXS + 1)
    rate_row = jax.random.randint(key_row, (V,), -MAXS, MAXS + 1)
    rate_col = rate_col.at[0].set(MAXS)
    rate_row = rate_row.at[0].set(-MAXS)
    stride = jax.random.randint(key_time, (EPOCHS - 1,), 1, 6)
    times = jnp.concatenate([jnp.zeros((1,), jnp.int32), jnp.cumsum(stride).astype(jnp.int32)])
    span = times[EPOCHS - 1]
    shift_col = rate_col[None, :] * times[:, None] // span
    shift_row = rate_row[None, :] * times[:, None] // span
    return jnp.stack([shift_col, shift_row], axis=0).astype(jnp.int32)


def levels(own_key, extent, split, least, largest):
    level = 1.0
    for axis_at, shards_of in split:
        draws = jax.random.uniform(jax.random.fold_in(jax.random.fold_in(own_key, 6), axis_at), (shards_of,), jnp.float32, least / len(split), largest / len(split))
        level = level * jnp.repeat(jnp.exp(draws), extent[axis_at] // shards_of).reshape((-1,) + (1,) * (len(extent) - 1 - axis_at))
    return level


def gaussian(rng, extent, width, reach, pieces=(), dtype=jnp.bfloat16):
    gain = levels(rng, extent, pieces, -0.22, 0.18) if pieces else 1.0
    result = jax.random.normal(rng, extent, jnp.float32) * width * gain
    return jnp.minimum(jnp.maximum(result, -reach), reach).astype(dtype)


def setup_inputs(seed: int = 0) -> dict:
    seeds = jax.random.split(jax.random.key(seed), 5)
    return {
        "science": gaussian(seeds[0], (EPOCHS, H, W), 1.0, 6.0, ((0, 4), (1, 8)), jnp.float32),
        "variance": jnp.clip(jnp.exp(math.log(4.0) - 2.7725887 * jax.random.uniform(seeds[1], (EPOCHS, H, W), jnp.float32) ** levels(seeds[1], (EPOCHS, H, W), ((0, 4), (1, 8)), -0.2, 0.2)), 0.25, 4.0),
        "psf": jnp.clip(jnp.exp(math.log(1.0) - 2.9957323 * jax.random.uniform(seeds[2], (EPOCHS, TAPS), jnp.float32) ** levels(seeds[2], (EPOCHS, TAPS), ((0, 4),), -0.2, 0.2)), 0.05, 1.0),
        "shifts": draw_shifts(jax.random.fold_in(seeds[4], 71), 0),
    }


def correlate(images, weights, axis):
    radius = weights.shape[-1] // 2
    length = images.shape[axis]
    margins = [(0, 0)] * images.ndim
    margins[axis] = (radius, radius)
    padded = jnp.pad(images, margins)
    summed = jnp.zeros_like(images)
    for offset in range(weights.shape[-1]):
        summed = summed + weights[:, :, offset, None, None] * lax.slice_in_dim(padded, offset, offset + length, axis=axis)
    return summed

def reference(science, variance, psf, shifts):
    pairing = jnp.stack([science / variance, 1.0 / variance], axis=1)
    weights = jnp.stack([psf, psf * psf], axis=1)
    filtered = correlate(correlate(pairing, weights, 3), weights, 2)
    padded = jnp.pad(filtered, ((0, 0), (0, 0), (MAXS, MAXS), (MAXS, MAXS)))
    rows_all = filtered.shape[2]
    cols_all = filtered.shape[3]

    def window_at(image, shift_col, shift_row):
        return lax.dynamic_slice(image, (jnp.int32(0), (MAXS + shift_row).astype(jnp.int32), (MAXS + shift_col).astype(jnp.int32)), (2, rows_all, cols_all))

    def likely(columns):
        stacked = lax.optimization_barrier(jnp.sum(jax.vmap(window_at)(padded, columns[0], columns[1]), axis=0))
        return stacked[0] / jnp.sqrt(stacked[1])
    return lax.map(likely, jnp.moveaxis(shifts, 2, 0))
```

```python
import functools

import jax
import jax.numpy as jnp
from jax import lax
from jax.experimental import pallas as pl
from jax.experimental.pallas import tpu as pltpu
from jax.sharding import PartitionSpec as P

VMEM = pl.BlockSpec(memory_space=pltpu.VMEM)
SMEM = pl.BlockSpec(memory_space=pltpu.SMEM)
LANES = 128


def columns_kernel(science_ref, variance_ref, psf_ref, out_ref):
    slots, height, breadth = science_ref.shape
    taps = psf_ref.shape[1]
    radius = taps // 2
    column = lax.broadcasted_iota(jnp.int32, (2 * height, breadth), 1)
    row = lax.broadcasted_iota(jnp.int32, (2 * height, 1), 0)
    for e in range(slots):
        inverse = 1.0 / variance_ref[e]
        pair = jnp.concatenate([science_ref[e] / variance_ref[e], inverse], axis=0)
        summed = jnp.zeros_like(pair)
        for k in range(taps):
            w = psf_ref[e, k]
            weight = jnp.where(row < height, w, w * w)
            reach = k - radius
            moved = pair
            if reach:
                moved = pltpu.roll(pair, (-reach) % breadth, 1)
                inside = column < breadth - reach if reach > 0 else column >= -reach
                moved = jnp.where(inside, moved, 0.0)
            summed = summed + weight * moved
        out_ref[e] = summed


def stack_kernel(order, place_ref, psf_ref, shifts_ref, *refs):
    pieces, outs = refs[:-order], refs[-order:]
    slots, paired, breadth = pieces[0].shape[-3:]
    height = paired // 2
    taps = psf_ref.shape[1]
    radius = taps // 2
    sources = sum(p.shape[0] for p in pieces)
    rows_all = sources * height
    block = rows_all // order
    epoch = place_ref[0]
    mine = place_ref[1]
    depth = sources * slots * paired
    lane = lax.broadcasted_iota(jnp.int32, (paired, LANES), 1)

    def shifted(x, shift):
        tiles = [x[:, i : i + LANES] for i in range(0, breadth, LANES)]
        turn = lax.rem(LANES - shift, LANES)
        turned = [pltpu.roll(t, turn, 1) for t in tiles]
        zero = jnp.zeros_like(turned[0])
        inside = (lane + shift >= 0) & (lane + shift < LANES)
        ahead = jnp.broadcast_to(shift >= 0, lane.shape)
        made = []
        for i, t in enumerate(turned):
            after = turned[i + 1] if i + 1 < len(turned) else zero
            before = turned[i - 1] if i else zero
            made.append(jnp.where(inside, t, jnp.where(ahead, after, before)))
        return jnp.concatenate(made, axis=1)

    images = []
    for p in pieces:
        for s in range(p.shape[0]):
            for e in range(slots):
                images.append(shifted(p[s, e], shifts_ref[0, epoch * slots + e, 0]))
    image = jnp.concatenate(images, axis=0)

    out_at = lax.broadcasted_iota(jnp.int32, (2 * rows_all, 1), 0)
    step = out_at // (2 * block)
    out_member = (out_at // block) % 2
    out_row = (step ^ epoch) * block + out_at % block
    in_at = lax.broadcasted_iota(jnp.int32, (1, depth), 1)
    in_row_local = in_at % height
    in_member = (in_at // height) % 2
    in_slot = (in_at // paired) % slots
    place = in_at // (paired * slots)
    in_source = jnp.zeros_like(place)
    for s in range(sources):
        in_source = jnp.where(place == s, mine ^ place_ref[2 + s], in_source)
    in_row = in_source * height + in_row_local
    shift_row = jnp.zeros_like(in_at)
    for e in range(slots):
        shift_row = jnp.where(in_slot == e, shifts_ref[1, epoch * slots + e, 0], shift_row)
    target = out_row + shift_row
    tap = in_row - target + radius
    matrix = jnp.zeros((2 * rows_all, depth), jnp.float32)
    for k in range(taps):
        weight = jnp.zeros(in_at.shape, jnp.float32)
        for e in range(slots):
            weight = jnp.where(in_slot == e, psf_ref[e, k], weight)
        weight = jnp.where(in_member == 0, weight, weight * weight)
        matrix = jnp.where(tap == k, weight, matrix)
    keep = (target >= 0) & (target < rows_all) & (in_member == out_member)
    matrix = jnp.where(keep, matrix, 0.0)
    product = jnp.dot(
        matrix, image, precision=lax.Precision.HIGHEST, preferred_element_type=jnp.float32
    )
    for k, out in enumerate(outs):
        for m in range(2):
            at = (2 * k + m) * block
            out[m] = product[at : at + block]


def exchange(array, axis, mask):
    count = lax.axis_size(axis)
    return lax.ppermute(array, axis, [(i, i ^ mask) for i in range(count)])


def per_device(science, variance, psf, shifts):
    slots, height, breadth = science.shape
    order = lax.axis_size("epoch")
    sources = lax.axis_size("vel")
    filtered = pl.pallas_call(
        columns_kernel,
        out_shape=jax.ShapeDtypeStruct((slots, 2 * height, breadth), jnp.float32),
        in_specs=[VMEM, VMEM, SMEM],
        out_specs=VMEM,
        name="columns",
    )(science, variance, psf)
    if sources <= 8:
        masks = list(range(0, sources, 2))
        same = jnp.stack([filtered] + [exchange(filtered, "vel", m) for m in masks[1:]])
        pieces = [same, exchange(same, "vel", 1)]
        masks = masks + [m ^ 1 for m in masks]
        mine = lax.axis_index("vel")
    else:
        pieces = [lax.all_gather(filtered, "vel")]
        masks = list(range(sources))
        mine = 0
    place = jnp.stack([jnp.int32(v) for v in [lax.axis_index("epoch"), mine] + masks])
    block = sources * height // order
    chunks = pl.pallas_call(
        functools.partial(stack_kernel, order),
        out_shape=[jax.ShapeDtypeStruct((2, block, breadth), jnp.float32)] * order,
        in_specs=[SMEM] * 3 + [VMEM] * len(pieces),
        out_specs=[VMEM] * order,
        name="stack",
    )(place, psf, shifts, *pieces)
    total = chunks[0]
    for k in range(1, order):
        total = total + exchange(chunks[k], "epoch", k)
    return (total[0] / jnp.sqrt(total[1]))[None]


def solution(mesh):
    return jax.shard_map(
        per_device,
        mesh=mesh,
        in_specs=(
            P("epoch", "vel", None),
            P("epoch", "vel", None),
            P("epoch", None),
            P(None, None, "vel"),
        ),
        out_specs=P("vel", "epoch", None),
        check_vma=False,
    )
```

```python
import functools

import jax
import jax.numpy as jnp
from jax import lax
from jax.experimental import pallas as pl
from jax.experimental.pallas import tpu as pltpu
from jax.sharding import PartitionSpec as P


VMEM = pl.BlockSpec(memory_space=pltpu.VMEM)
SMEM = pl.BlockSpec(memory_space=pltpu.SMEM)
HBM = pl.BlockSpec(memory_space=pltpu.HBM)
LANES = 128


def tiles_of(x):
    return [x[:, i : i + LANES] for i in range(0, x.shape[1], LANES)]


def columns_kernel(science_hbm, variance_hbm, psf_hbm, out_ref, science, variance, psf, sems):
    copies = [
        pltpu.make_async_copy(source, target, sems.at[i])
        for i, (source, target) in enumerate(
            ((variance_hbm, variance), (science_hbm, science), (psf_hbm, psf))
        )
    ]
    for copy in copies:
        copy.start()
    slots, height, _ = science.shape
    taps = psf.shape[1]
    radius = taps // 2
    lane = lax.broadcasted_iota(jnp.int32, (2 * height, LANES), 1)
    psi_row = lax.broadcasted_iota(jnp.int32, (2 * height, LANES), 0) < height
    for copy in copies:
        copy.wait()
    for e in range(slots):
        inverse = 1.0 / variance[e]
        pair = tiles_of(jnp.concatenate([science[e] * inverse, inverse], axis=0))
        zero = jnp.zeros_like(pair[0])
        summed = [zero] * len(pair)
        for k in range(taps):
            w = psf[e, k]
            weight = jnp.where(psi_row, w, w * w)
            reach = k - radius
            moved = pair
            if reach:
                turned = [pltpu.roll(t, (-reach) % LANES, 1) for t in pair]
                if reach > 0:
                    moved = [jnp.where(lane < LANES - reach, a, b) for a, b in zip(turned, turned[1:] + [zero])]
                else:
                    moved = [jnp.where(lane >= -reach, a, b) for a, b in zip(turned, [zero] + turned[:-1])]
            summed = [s + weight * m for s, m in zip(summed, moved)]
        out_ref[e] = jnp.concatenate(summed, axis=1)


def banded(order, masks, relative, height, slots, psf_ref, shifts_ref):
    taps = psf_ref.shape[1]
    radius = taps // 2
    sources = len(masks)
    paired = 2 * height
    rows_all = sources * height
    block = rows_all // order
    depth = sources * slots * paired
    epoch = lax.axis_index("epoch")
    mine = lax.axis_index("vel") if relative else 0
    out_at = lax.broadcasted_iota(jnp.int32, (2 * rows_all, 1), 0)
    step = out_at // (2 * block)
    out_member = (out_at // block) % 2
    out_row = (step ^ epoch) * block + out_at % block
    in_at = lax.broadcasted_iota(jnp.int32, (1, depth), 1)
    in_member = (in_at // height) % 2
    in_slot = (in_at // paired) % slots
    place = in_at // (paired * slots)
    in_source = jnp.zeros_like(place)
    for s, mask in enumerate(masks):
        in_source = jnp.where(place == s, mine ^ mask, in_source)
    in_row = in_source * height + in_at % height
    shift_row = jnp.zeros_like(in_at)
    for e in range(slots):
        shift_row = jnp.where(in_slot == e, shifts_ref[1, epoch * slots + e], shift_row)
    target = out_row + shift_row
    tap = in_row - target + radius
    matrix = jnp.zeros((2 * rows_all, depth), jnp.float32)
    for k in range(taps):
        weight = jnp.zeros(in_at.shape, jnp.float32)
        for e in range(slots):
            weight = jnp.where(in_slot == e, psf_ref[e, k], weight)
        weight = jnp.where(in_member == 0, weight, weight * weight)
        matrix = jnp.where(tap == k, weight, matrix)
    keep = (target >= 0) & (target < rows_all) & (in_member == out_member)
    return jnp.where(keep, matrix, 0.0)


def split(x):
    high = x.astype(jnp.bfloat16)
    return high, (x - high.astype(jnp.float32)).astype(jnp.bfloat16)


def shifted(x, shift):
    tiles = tiles_of(x)
    lane = lax.broadcasted_iota(jnp.int32, tiles[0].shape, 1)
    turned = [pltpu.roll(t, lax.rem(LANES - shift, LANES), 1) for t in tiles]
    zero = jnp.zeros_like(turned[0])
    inside = (lane + shift >= 0) & (lane + shift < LANES)
    ahead = jnp.broadcast_to(shift, lane.shape) >= 0
    made = []
    for before, t, after in zip([zero] + turned[:-1], turned, turned[1:] + [zero]):
        made.append(jnp.where(inside, t, jnp.where(ahead, after, before)))
    return jnp.concatenate(made, axis=1)


def product_of(pieces, shifts, high, low):
    images = [shifted(p[s, e], shift) for p in pieces for s in range(p.shape[0]) for e, shift in enumerate(shifts)]
    image_high, image_low = split(jnp.concatenate(images, axis=0))
    dot = functools.partial(jnp.dot, preferred_element_type=jnp.float32)
    return dot(high, image_high) + dot(high, image_low) + dot(low, image_high)


def store_blocks(product, outs):
    at = 0
    for out in outs:
        rows = out.shape[-2]
        for m in range(out.shape[0]):
            out[m] = product[at : at + rows]
            at += rows


def matrix_kernel(order, masks, height, psf_ref, shifts_ref, high_ref, low_ref, column_ref):
    slots = column_ref.shape[0]
    matrix = banded(order, masks, True, height, slots, psf_ref, shifts_ref)
    high_ref[...], low_ref[...] = split(matrix)
    epoch = lax.axis_index("epoch")
    for e in range(slots):
        shift = shifts_ref[0, epoch * slots + e]
        column_ref[e] = jnp.full(column_ref.shape[1:], shift, jnp.int32)


def partial_product(pieces, start, high_ref, low_ref, column_ref):
    slots, paired = pieces[0].shape[1:3]
    stop = start + sum(p.shape[0] for p in pieces) * slots * paired
    shifts = [column_ref[e][0, 0] for e in range(slots)]
    return product_of(pieces, shifts, high_ref[:, start:stop], low_ref[:, start:stop])


def early_kernel(high_ref, low_ref, column_ref, pieces_ref, partial_ref):
    partial_ref[...] = partial_product([pieces_ref], 0, high_ref, low_ref, column_ref)


def late_kernel(high_ref, low_ref, column_ref, partial_ref, pieces_ref, *outs):
    start = high_ref.shape[1] // 2
    product = partial_product([pieces_ref], start, high_ref, low_ref, column_ref)
    store_blocks(partial_ref[...] + product, outs)


def whole_kernel(order, masks, psf_ref, shifts_ref, pieces_ref, *outs):
    slots, paired = pieces_ref.shape[1:3]
    high, low = split(banded(order, masks, False, paired // 2, slots, psf_ref, shifts_ref))
    epoch = lax.axis_index("epoch")
    shifts = [shifts_ref[0, epoch * slots + e] for e in range(slots)]
    store_blocks(product_of([pieces_ref], shifts, high, low), outs)


def grant(bytes_used):
    return pltpu.CompilerParams(vmem_limit_bytes=min(4 * bytes_used, 60 << 20))


def exchange(array, axis, mask):
    count = lax.axis_size(axis)
    return lax.ppermute(array, axis, [(i, i ^ mask) for i in range(count)])


def per_device(science, variance, psf, shifts):
    slots, height, breadth = science.shape
    order = lax.axis_size("epoch")
    sources = lax.axis_size("vel")
    paired = 2 * height
    shifts = shifts.reshape(shifts.shape[:2])
    filtered = pl.pallas_call(
        columns_kernel,
        out_shape=jax.ShapeDtypeStruct((slots, paired, breadth), jnp.float32),
        in_specs=[HBM, HBM, HBM],
        out_specs=VMEM,
        scratch_shapes=[
            pltpu.VMEM(science.shape, jnp.float32),
            pltpu.VMEM(science.shape, jnp.float32),
            pltpu.SMEM(psf.shape, jnp.float32),
            pltpu.SemaphoreType.DMA((3,)),
        ],
        compiler_params=grant(16 * science.size),
        name="columns",
    )(*(pltpu.with_memory_space_constraint(a, pltpu.HBM) for a in (science, variance, psf)))
    rows_all = sources * height
    block = rows_all // order
    depth = sources * slots * paired
    used = grant(4 * (sources * filtered.size + 2 * rows_all * (depth + breadth)))
    chunk = jax.ShapeDtypeStruct((2, block, breadth), jnp.float32)
    if sources == 8:
        across = exchange(filtered, "vel", 6)
        along = exchange(filtered, "vel", 4)
        aside = exchange(filtered, "vel", 2)
        own = jnp.stack([filtered, across, along, aside])
        twin = exchange(own, "vel", 1)
        masks = [0, 6, 4, 2, 1, 7, 5, 3]
        state = pl.pallas_call(
            functools.partial(matrix_kernel, order, masks, height),
            out_shape=[
                jax.ShapeDtypeStruct((2 * rows_all, depth), jnp.bfloat16),
                jax.ShapeDtypeStruct((2 * rows_all, depth), jnp.bfloat16),
                jax.ShapeDtypeStruct((slots, 8, LANES), jnp.int32),
            ],
            in_specs=[SMEM] * 2,
            out_specs=[VMEM] * 3,
            compiler_params=used,
            name="matrix",
        )(psf, shifts)
        partial = pl.pallas_call(
            early_kernel,
            out_shape=jax.ShapeDtypeStruct((2 * rows_all, breadth), jnp.float32),
            in_specs=[VMEM] * 4,
            out_specs=VMEM,
            compiler_params=used,
            name="early",
        )(*state, own)
        chunks = pl.pallas_call(
            late_kernel,
            out_shape=[chunk] * order,
            in_specs=[VMEM] * 5,
            out_specs=[VMEM] * order,
            compiler_params=used,
            name="late",
        )(*state, partial, twin)
    else:
        chunks = pl.pallas_call(
            functools.partial(whole_kernel, order, list(range(sources))),
            out_shape=[chunk] * order,
            in_specs=[SMEM] * 2 + [VMEM],
            out_specs=[VMEM] * order,
            compiler_params=used,
            name="stack",
        )(psf, shifts, lax.all_gather(filtered, "vel"))
    terms = [chunks[0]] + [exchange(chunks[k], "epoch", k) for k in range(1, order)]
    psi, phi = (sum(t[m] for t in terms) for m in range(2))
    return (psi / jnp.sqrt(phi))[None]


def solution(mesh):
    return jax.shard_map(
        per_device,
        mesh=mesh,
        in_specs=(
            P("epoch", "vel", None),
            P("epoch", "vel", None),
            P("epoch", None),
            P(None, None, "vel"),
        ),
        out_specs=P("vel", "epoch", None),
        check_vma=False,
    )
```

```python
import functools

import jax
import jax.numpy as jnp
from jax import lax
from jax.experimental import pallas as pl
from jax.experimental.pallas import tpu as pltpu
from jax.sharding import PartitionSpec as P


VMEM = pl.BlockSpec(memory_space=pltpu.VMEM)
SMEM = pl.BlockSpec(memory_space=pltpu.SMEM)
HBM = pl.BlockSpec(memory_space=pltpu.HBM)
LANES = 128
ROUNDS = ((1, 2, 3, 0), (3, 0, 1, 2), (2, 3, 0, 1))
RING = (0, 1, 3, 2)


def tiles_of(x):
    return [x[:, i : i + LANES] for i in range(0, x.shape[1], LANES)]


def columns_kernel(science_hbm, variance_hbm, psf_hbm, out_ref, science, variance, psf, sems):
    copies = [
        pltpu.make_async_copy(source, target, sems.at[i])
        for i, (source, target) in enumerate(
            ((variance_hbm, variance), (science_hbm, science), (psf_hbm, psf))
        )
    ]
    for copy in copies:
        copy.start()
    slots, height, _ = science.shape
    taps = psf.shape[1]
    radius = taps // 2
    lane = lax.broadcasted_iota(jnp.int32, (2 * height, LANES), 1)
    psi_row = lax.broadcasted_iota(jnp.int32, (2 * height, LANES), 0) < height
    for copy in copies:
        copy.wait()
    for e in range(slots):
        inverse = 1.0 / variance[e]
        pair = tiles_of(jnp.concatenate([science[e] * inverse, inverse], axis=0))
        zero = jnp.zeros_like(pair[0])
        summed = [zero] * len(pair)
        for k in range(taps):
            w = psf[e, k]
            weight = jnp.where(psi_row, w, w * w)
            reach = k - radius
            moved = pair
            if reach:
                turned = [pltpu.roll(t, (-reach) % LANES, 1) for t in pair]
                if reach > 0:
                    moved = [jnp.where(lane < LANES - reach, a, b) for a, b in zip(turned, turned[1:] + [zero])]
                else:
                    moved = [jnp.where(lane >= -reach, a, b) for a, b in zip(turned, [zero] + turned[:-1])]
            summed = [s + weight * m for s, m in zip(summed, moved)]
        out_ref[e] = jnp.concatenate(summed, axis=1)


def chosen(values, index):
    if len(set(values)) == 1:
        return jnp.int32(values[0])
    return sum(jnp.where(index == i, jnp.int32(v), 0) for i, v in enumerate(values))


def banded(ring, origins, height, slots, psf_ref, shifts_ref):
    taps = psf_ref.shape[1]
    radius = taps // 2
    sources = len(origins)
    paired = 2 * height
    rows_all = sources * height
    order = len(ring)
    block = rows_all // order
    depth = sources * slots * paired
    epoch = lax.axis_index("epoch")
    mine = lax.axis_index("vel")
    out_at = lax.broadcasted_iota(jnp.int32, (2 * rows_all, 1), 0)
    step = out_at // (2 * block)
    out_member = (out_at // block) % 2
    out_block = jnp.zeros_like(step)
    for k in range(order):
        target = chosen([target_of(ring, k, i) for i in range(order)], epoch)
        out_block = jnp.where(step == k, target, out_block)
    out_row = out_block * block + out_at % block
    in_at = lax.broadcasted_iota(jnp.int32, (1, depth), 1)
    in_member = (in_at // height) % 2
    in_slot = (in_at // paired) % slots
    place = in_at // (paired * slots)
    in_source = jnp.zeros_like(place)
    for s, row in enumerate(origins):
        in_source = jnp.where(place == s, chosen(row, mine), in_source)
    in_row = in_source * height + in_at % height
    shift_row = jnp.zeros_like(in_at)
    for e in range(slots):
        shift_row = jnp.where(in_slot == e, shifts_ref[1, epoch * slots + e], shift_row)
    target = out_row + shift_row
    tap = in_row - target + radius
    matrix = jnp.zeros((2 * rows_all, depth), jnp.float32)
    for k in range(taps):
        weight = jnp.zeros(in_at.shape, jnp.float32)
        for e in range(slots):
            weight = jnp.where(in_slot == e, psf_ref[e, k], weight)
        weight = jnp.where(in_member == 0, weight, weight * weight)
        matrix = jnp.where(tap == k, weight, matrix)
    keep = (target >= 0) & (target < rows_all) & (in_member == out_member)
    return jnp.where(keep, matrix, 0.0)


def split(x):
    high = x.astype(jnp.bfloat16)
    return high, (x - high.astype(jnp.float32)).astype(jnp.bfloat16)


def shifted(x, shift):
    tiles = tiles_of(x)
    lane = lax.broadcasted_iota(jnp.int32, tiles[0].shape, 1)
    turned = [pltpu.roll(t, lax.rem(LANES - shift, LANES), 1) for t in tiles]
    zero = jnp.zeros_like(turned[0])
    inside = (lane + shift >= 0) & (lane + shift < LANES)
    ahead = jnp.broadcast_to(shift, lane.shape) >= 0
    made = []
    for before, t, after in zip([zero] + turned[:-1], turned, turned[1:] + [zero]):
        made.append(jnp.where(inside, t, jnp.where(ahead, after, before)))
    return jnp.concatenate(made, axis=1)


def parts_of(matrix):
    high, low = split(matrix)
    return jnp.concatenate([high, high, low], axis=1)


def product_of(parts, pieces, shifts):
    images = [shifted(p[s, e], shift) for p in pieces for s in range(p.shape[0]) for e, shift in enumerate(shifts)]
    high, low = split(jnp.concatenate(images, axis=0))
    return jnp.dot(parts, jnp.concatenate([high, low, high], axis=0), preferred_element_type=jnp.float32)


def store_blocks(product, outs):
    at = 0
    for out in outs:
        rows = out.shape[-2]
        for m in range(out.shape[0]):
            out[m] = product[at : at + rows]
            at += rows


def matrix_kernel(ring, origins, height, psf_ref, shifts_ref, column_ref, *parts_refs):
    slots = column_ref.shape[0]
    matrix = banded(ring, origins, height, slots, psf_ref, shifts_ref)
    at = 0
    for ref in parts_refs:
        depth = ref.shape[1] // 3
        ref[...] = parts_of(matrix[:, at : at + depth])
        at += depth
    epoch = lax.axis_index("epoch")
    for e in range(slots):
        shift = shifts_ref[0, epoch * slots + e]
        column_ref[e] = jnp.full(column_ref.shape[1:], shift, jnp.int32)


def stack_kernel(count, added, column_ref, parts_ref, *refs):
    pieces, refs = refs[:count], refs[count:]
    shifts = [column_ref[e][0, 0] for e in range(column_ref.shape[0])]
    product = product_of(parts_ref[...], pieces, shifts)
    if added:
        product, refs = refs[0][...] + product, refs[1:]
    if len(refs) == 1:
        refs[0][...] = product
    else:
        store_blocks(product, refs)


def whole_kernel(ring, origins, psf_ref, shifts_ref, pieces_ref, *outs):
    slots, paired = pieces_ref.shape[1:3]
    parts = parts_of(banded(ring, origins, paired // 2, slots, psf_ref, shifts_ref))
    epoch = lax.axis_index("epoch")
    shifts = [shifts_ref[0, epoch * slots + e] for e in range(slots)]
    store_blocks(product_of(parts, [pieces_ref], shifts), outs)


def grant(bytes_used):
    return pltpu.CompilerParams(vmem_limit_bytes=min(4 * bytes_used, 60 << 20))


def send(array, axis, targets):
    return lax.ppermute(array, axis, list(enumerate(targets)))


def target_of(ring, step, device):
    return ring[(ring.index(device) + step) % len(ring)]


def rotate(array, axis, ring, step):
    return lax.ppermute(array, axis, [(i, target_of(ring, step, i)) for i in ring])


def per_device(science, variance, psf, shifts):
    slots, height, breadth = science.shape
    order = lax.axis_size("epoch")
    sources = lax.axis_size("vel")
    ring = RING if order == len(RING) else tuple(range(order))
    paired = 2 * height
    shifts = shifts.reshape(shifts.shape[:2])
    filtered = pl.pallas_call(
        columns_kernel,
        out_shape=jax.ShapeDtypeStruct((slots, paired, breadth), jnp.float32),
        in_specs=[HBM, HBM, HBM],
        out_specs=VMEM,
        scratch_shapes=[
            pltpu.VMEM(science.shape, jnp.float32),
            pltpu.VMEM(science.shape, jnp.float32),
            pltpu.SMEM(psf.shape, jnp.float32),
            pltpu.SemaphoreType.DMA((3,)),
        ],
        compiler_params=grant(16 * science.size),
        name="columns",
    )(*(pltpu.with_memory_space_constraint(a, pltpu.HBM) for a in (science, variance, psf)))
    rows_all = sources * height
    block = rows_all // order
    depth = sources * slots * paired
    used = grant(4 * (sources * filtered.size + 2 * rows_all * (depth + breadth)))
    chunk = jax.ShapeDtypeStruct((2, block, breadth), jnp.float32)
    if sources == 2 * len(ROUNDS[0]):
        rounds = [[2 * t + c for t in targets for c in range(2)] for targets in ROUNDS]
        arrived = [send(filtered, "vel", targets) for targets in rounds]
        own = jnp.stack([filtered] + arrived[:-1])
        last = arrived[-1][None]
        sibling = [v ^ 1 for v in range(sources)]
        twin = send(own, "vel", sibling)
        twin_last = send(last, "vel", sibling)
        origins = [list(range(sources))] + [[t.index(v) for v in range(sources)] for t in rounds]
        origins = origins + [[row[v ^ 1] for v in range(sources)] for row in origins]
        groups = [[own, last], [twin], [twin_last]]
        depths = [sum(p.shape[0] for p in g) * slots * paired for g in groups]
        column, *parts = pl.pallas_call(
            functools.partial(matrix_kernel, ring, origins, height),
            out_shape=[jax.ShapeDtypeStruct((slots, 8, LANES), jnp.int32)]
            + [jax.ShapeDtypeStruct((2 * rows_all, 3 * d), jnp.bfloat16) for d in depths],
            in_specs=[SMEM] * 2,
            out_specs=[VMEM] * (1 + len(depths)),
            compiler_params=used,
            name="matrix",
        )(psf, shifts)
        partial = []
        for name, group, left in zip(("early", "middle", "late"), groups, parts):
            shapes = [jax.ShapeDtypeStruct((2 * rows_all, breadth), jnp.float32)]
            if name == "late":
                shapes = [chunk] * order
            operands = [column, left, *group, *partial]
            partial = pl.pallas_call(
                functools.partial(stack_kernel, len(group), bool(partial)),
                out_shape=shapes,
                in_specs=[VMEM] * len(operands),
                out_specs=[VMEM] * len(shapes),
                compiler_params=used,
            )(*operands)
        chunks = partial
    else:
        chunks = pl.pallas_call(
            functools.partial(whole_kernel, ring, [[s] * sources for s in range(sources)]),
            out_shape=[chunk] * order,
            in_specs=[SMEM] * 2 + [VMEM],
            out_specs=[VMEM] * order,
            compiler_params=used,
            name="stack",
        )(psf, shifts, lax.all_gather(filtered, "vel"))
    terms = [chunks[0]] + [rotate(chunks[k], "epoch", ring, k) for k in range(1, order)]
    psi, phi = (sum(t[m] for t in terms) for m in range(2))
    return (psi / jnp.sqrt(phi))[None]


def solution(mesh):
    return jax.shard_map(
        per_device,
        mesh=mesh,
        in_specs=(
            P("epoch", "vel", None),
            P("epoch", "vel", None),
            P("epoch", None),
            P(None, None, "vel"),
        ),
        out_specs=P("vel", "epoch", None),
        check_vma=False,
    )
```

```python
import functools

import jax
import jax.numpy as jnp
from jax import lax
from jax.experimental import pallas as pl
from jax.experimental.pallas import tpu as pltpu
from jax.sharding import PartitionSpec as P


VMEM = pl.BlockSpec(memory_space=pltpu.VMEM)
SMEM = pl.BlockSpec(memory_space=pltpu.SMEM)
HBM = pl.BlockSpec(memory_space=pltpu.HBM)
LANES = 128
ROUNDS = ((1, 2, 3, 0), (3, 0, 1, 2), (2, 3, 0, 1))
STEPS = ((1, 2, 0, 3), (2, 3, 1, 0), (3, 0, 2, 1), (0, 1, 3, 2))


def tiles_of(x):
    return [x[:, i : i + LANES] for i in range(0, x.shape[1], LANES)]


def columns_kernel(science_hbm, variance_hbm, psf_hbm, out_ref, science, variance, psf, sems):
    copies = [
        pltpu.make_async_copy(source, target, sems.at[i])
        for i, (source, target) in enumerate(
            ((variance_hbm, variance), (science_hbm, science), (psf_hbm, psf))
        )
    ]
    for copy in copies:
        copy.start()
    slots, height, _ = science.shape
    taps = psf.shape[1]
    radius = taps // 2
    lane = lax.broadcasted_iota(jnp.int32, (2 * height, LANES), 1)
    psi_row = lax.broadcasted_iota(jnp.int32, (2 * height, LANES), 0) < height
    for copy in copies:
        copy.wait()
    for e in range(slots):
        inverse = 1.0 / variance[e]
        pair = tiles_of(jnp.concatenate([science[e] * inverse, inverse], axis=0))
        zero = jnp.zeros_like(pair[0])
        summed = [zero] * len(pair)
        for k in range(taps):
            w = psf[e, k]
            weight = jnp.where(psi_row, w, w * w)
            reach = k - radius
            moved = pair
            if reach:
                turned = [pltpu.roll(t, (-reach) % LANES, 1) for t in pair]
                if reach > 0:
                    moved = [jnp.where(lane < LANES - reach, a, b) for a, b in zip(turned, turned[1:] + [zero])]
                else:
                    moved = [jnp.where(lane >= -reach, a, b) for a, b in zip(turned, [zero] + turned[:-1])]
            summed = [s + weight * m for s, m in zip(summed, moved)]
        out_ref[e] = jnp.concatenate(summed, axis=1)


def chosen(values, index):
    if len(set(values)) == 1:
        return jnp.int32(values[0])
    return sum(jnp.where(index == i, jnp.int32(v), 0) for i, v in enumerate(values))


def banded(steps, origins, height, slots, psf_ref, shifts_ref):
    taps = psf_ref.shape[1]
    radius = taps // 2
    sources = len(origins)
    paired = 2 * height
    rows_all = sources * height
    order = len(steps)
    block = rows_all // order
    depth = sources * slots * paired
    epoch = lax.axis_index("epoch")
    mine = lax.axis_index("vel")
    out_at = lax.broadcasted_iota(jnp.int32, (2 * rows_all, 1), 0)
    step = out_at // (2 * block)
    out_member = (out_at // block) % 2
    out_block = jnp.zeros_like(step)
    for k in range(order):
        target = chosen(steps[k], epoch)
        out_block = jnp.where(step == k, target, out_block)
    out_row = out_block * block + out_at % block
    in_at = lax.broadcasted_iota(jnp.int32, (1, depth), 1)
    in_member = (in_at // height) % 2
    in_slot = (in_at // paired) % slots
    place = in_at // (paired * slots)
    in_source = jnp.zeros_like(place)
    for s, row in enumerate(origins):
        in_source = jnp.where(place == s, chosen(row, mine), in_source)
    in_row = in_source * height + in_at % height
    shift_row = jnp.zeros_like(in_at)
    for e in range(slots):
        shift_row = jnp.where(in_slot == e, shifts_ref[1, epoch * slots + e], shift_row)
    target = out_row + shift_row
    tap = in_row - target + radius
    matrix = jnp.zeros((2 * rows_all, depth), jnp.float32)
    for k in range(taps):
        weight = jnp.zeros(in_at.shape, jnp.float32)
        for e in range(slots):
            weight = jnp.where(in_slot == e, psf_ref[e, k], weight)
        weight = jnp.where(in_member == 0, weight, weight * weight)
        matrix = jnp.where(tap == k, weight, matrix)
    keep = (target >= 0) & (target < rows_all) & (in_member == out_member)
    return jnp.where(keep, matrix, 0.0)


def split(x):
    high = x.astype(jnp.bfloat16)
    return high, (x - high.astype(jnp.float32)).astype(jnp.bfloat16)


def shifted(x, shift):
    tiles = tiles_of(x)
    lane = lax.broadcasted_iota(jnp.int32, tiles[0].shape, 1)
    turned = [pltpu.roll(t, lax.rem(LANES - shift, LANES), 1) for t in tiles]
    zero = jnp.zeros_like(turned[0])
    inside = (lane + shift >= 0) & (lane + shift < LANES)
    ahead = jnp.broadcast_to(shift, lane.shape) >= 0
    made = []
    for before, t, after in zip([zero] + turned[:-1], turned, turned[1:] + [zero]):
        made.append(jnp.where(inside, t, jnp.where(ahead, after, before)))
    return jnp.concatenate(made, axis=1)


def parts_of(matrix):
    high, low = split(matrix)
    return jnp.concatenate([high, high, low], axis=1)


def product_of(parts, pieces, shifts):
    images = [shifted(p[s, e], shift) for p in pieces for s in range(p.shape[0]) for e, shift in enumerate(shifts)]
    high, low = split(jnp.concatenate(images, axis=0))
    return jnp.dot(parts, jnp.concatenate([high, low, high], axis=0), preferred_element_type=jnp.float32)


def store_blocks(product, outs):
    at = 0
    for out in outs:
        rows = out.shape[-2]
        for m in range(out.shape[0]):
            out[m] = product[at : at + rows]
            at += rows


def matrix_kernel(steps, origins, height, psf_ref, shifts_ref, column_ref, *parts_refs):
    slots = column_ref.shape[0]
    matrix = banded(steps, origins, height, slots, psf_ref, shifts_ref)
    at = 0
    for ref in parts_refs:
        depth = ref.shape[1] // 3
        ref[...] = parts_of(matrix[:, at : at + depth])
        at += depth
    epoch = lax.axis_index("epoch")
    for e in range(slots):
        shift = shifts_ref[0, epoch * slots + e]
        column_ref[e] = jnp.full(column_ref.shape[1:], shift, jnp.int32)


def stack_kernel(count, added, column_ref, parts_ref, *refs):
    pieces, refs = refs[:count], refs[count:]
    shifts = [column_ref[e][0, 0] for e in range(column_ref.shape[0])]
    product = product_of(parts_ref[...], pieces, shifts)
    if added:
        product, refs = refs[0][...] + product, refs[1:]
    if len(refs) == 1:
        refs[0][...] = product
    else:
        store_blocks(product, refs)


def whole_kernel(steps, origins, psf_ref, shifts_ref, pieces_ref, *outs):
    slots, paired = pieces_ref.shape[1:3]
    parts = parts_of(banded(steps, origins, paired // 2, slots, psf_ref, shifts_ref))
    epoch = lax.axis_index("epoch")
    shifts = [shifts_ref[0, epoch * slots + e] for e in range(slots)]
    store_blocks(product_of(parts, [pieces_ref], shifts), outs)


def grant(bytes_used):
    return pltpu.CompilerParams(vmem_limit_bytes=min(4 * bytes_used, 60 << 20))


def send(array, axis, targets):
    return lax.ppermute(array, axis, list(enumerate(targets)))


def hand(array, targets, grid):
    pairs = []
    for i, t in enumerate(targets):
        for v in range(grid):
            pairs.append((i * grid + v, t * grid + (v ^ 1 if t == i else v)))
    return lax.ppermute(array, ("epoch", "vel"), pairs)


def per_device(science, variance, psf, shifts):
    slots, height, breadth = science.shape
    order = lax.axis_size("epoch")
    sources = lax.axis_size("vel")
    steps = STEPS
    if order != len(STEPS):
        steps = [[(i + k) % order for i in range(order)] for k in range(order)]
    paired = 2 * height
    shifts = shifts.reshape(shifts.shape[:2])
    filtered = pl.pallas_call(
        columns_kernel,
        out_shape=jax.ShapeDtypeStruct((slots, paired, breadth), jnp.float32),
        in_specs=[HBM, HBM, HBM],
        out_specs=VMEM,
        scratch_shapes=[
            pltpu.VMEM(science.shape, jnp.float32),
            pltpu.VMEM(science.shape, jnp.float32),
            pltpu.SMEM(psf.shape, jnp.float32),
            pltpu.SemaphoreType.DMA((3,)),
        ],
        compiler_params=grant(16 * science.size),
        name="columns",
    )(*(pltpu.with_memory_space_constraint(a, pltpu.HBM) for a in (science, variance, psf)))
    rows_all = sources * height
    block = rows_all // order
    depth = sources * slots * paired
    used = grant(4 * (sources * filtered.size + 2 * rows_all * (depth + breadth)))
    chunk = jax.ShapeDtypeStruct((2, block, breadth), jnp.float32)
    if sources == 2 * len(ROUNDS[0]):
        rounds = [[2 * t + c for t in targets for c in range(2)] for targets in ROUNDS]
        arrived = [send(filtered, "vel", targets) for targets in rounds]
        own = jnp.stack([filtered] + arrived[:-1])
        last = arrived[-1][None]
        sibling = [v ^ 1 for v in range(sources)]
        twin = send(own, "vel", sibling)
        twin_last = send(last, "vel", sibling)
        origins = [list(range(sources))] + [[t.index(v) for v in range(sources)] for t in rounds]
        origins = origins + [[row[v ^ 1] for v in range(sources)] for row in origins]
        groups = [[own, last], [twin], [twin_last]]
        depths = [sum(p.shape[0] for p in g) * slots * paired for g in groups]
        column, *parts = pl.pallas_call(
            functools.partial(matrix_kernel, steps, origins, height),
            out_shape=[jax.ShapeDtypeStruct((slots, 8, LANES), jnp.int32)]
            + [jax.ShapeDtypeStruct((2 * rows_all, 3 * d), jnp.bfloat16) for d in depths],
            in_specs=[SMEM] * 2,
            out_specs=[VMEM] * (1 + len(depths)),
            compiler_params=used,
            name="matrix",
        )(psf, shifts)
        partial = []
        for name, group, left in zip(("early", "middle", "late"), groups, parts):
            shapes = [jax.ShapeDtypeStruct((2 * rows_all, breadth), jnp.float32)]
            if name == "late":
                shapes = [chunk] * order
            operands = [column, left, *group, *partial]
            partial = pl.pallas_call(
                functools.partial(stack_kernel, len(group), bool(partial)),
                out_shape=shapes,
                in_specs=[VMEM] * len(operands),
                out_specs=[VMEM] * len(shapes),
                compiler_params=used,
            )(*operands)
        chunks = partial
    else:
        chunks = pl.pallas_call(
            functools.partial(whole_kernel, steps, [[s] * sources for s in range(sources)]),
            out_shape=[chunk] * order,
            in_specs=[SMEM] * 2 + [VMEM],
            out_specs=[VMEM] * order,
            compiler_params=used,
            name="stack",
        )(psf, shifts, lax.all_gather(filtered, "vel"))
    terms = []
    for k, targets in enumerate(steps):
        came = hand(chunks[k], targets, sources)
        kept = chosen([int(t == i) for i, t in enumerate(targets)], lax.axis_index("epoch"))
        terms.append(jnp.where(kept == 1, chunks[k], came))
    psi, phi = (sum(t[m] for t in terms) for m in range(2))
    return (psi / jnp.sqrt(phi))[None]


def solution(mesh):
    return jax.shard_map(
        per_device,
        mesh=mesh,
        in_specs=(
            P("epoch", "vel", None),
            P("epoch", "vel", None),
            P("epoch", None),
            P(None, None, "vel"),
        ),
        out_specs=P("vel", "epoch", None),
        check_vma=False,
    )
```

```python
import functools

import jax
import jax.numpy as jnp
from jax import lax
from jax.experimental import pallas as pl
from jax.experimental.pallas import tpu as pltpu
from jax.sharding import PartitionSpec as P


VMEM = pl.BlockSpec(memory_space=pltpu.VMEM)
SMEM = pl.BlockSpec(memory_space=pltpu.SMEM)
HBM = pl.BlockSpec(memory_space=pltpu.HBM)
LANES = 128
ROUNDS = ((1, 2, 3, 0), (3, 0, 1, 2), (2, 3, 0, 1))
STEPS = ((1, 2, 0, 3), (2, 3, 1, 0), (3, 0, 2, 1), (0, 1, 3, 2))


def tiles_of(x):
    return [x[:, i : i + LANES] for i in range(0, x.shape[1], LANES)]


def moved(tiles, first, reach, lane, count):
    if not reach:
        return tiles[first : first + count]
    turned = [pltpu.roll(t, (-reach) % LANES, 1) for t in tiles]
    made = []
    for i in range(first, first + count):
        if reach > 0:
            other = turned[i + 1] if i + 1 < len(turned) else jnp.zeros_like(turned[i])
            made.append(jnp.where(lane < LANES - reach, turned[i], other))
        else:
            other = turned[i - 1] if i else jnp.zeros_like(turned[i])
            made.append(jnp.where(lane >= -reach, turned[i], other))
    return made


def columns_kernel(science_hbm, variance_hbm, psf_hbm, out_ref, science, variance, psf, sems):
    copies = [
        pltpu.make_async_copy(source, target, sems.at[i])
        for i, (source, target) in enumerate(
            ((psf_hbm, psf), (variance_hbm, variance), (science_hbm, science))
        )
    ]
    for copy in copies:
        copy.start()
    slots, height, _ = science.shape
    taps = psf.shape[1]
    inner = 3 if taps % 6 == 3 else 1
    outer = taps // inner
    lane = lax.broadcasted_iota(jnp.int32, (2 * height, LANES), 1)
    psi_row = lax.broadcasted_iota(jnp.int32, (2 * height, LANES), 0) < height
    for copy in copies[1:]:
        copy.wait()
    pairs = []
    for e in range(slots):
        inverse = 1.0 / variance[e]
        pairs.append(jnp.concatenate([science[e] * inverse, inverse], axis=0))
    copies[0].wait()
    for e, pair in enumerate(pairs):
        zero = jnp.zeros((2 * height, LANES), jnp.float32)
        tiles = [zero] + tiles_of(pair) + [zero]
        count = len(tiles)
        near = [moved(tiles, 0, i - inner // 2, lane, count) for i in range(inner)]
        summed = None
        for j in range(outer):
            group = None
            for i in range(inner):
                w = psf[e, j * inner + i]
                weight = jnp.where(psi_row, w, w * w)
                terms = [weight * t for t in near[i]]
                group = terms if group is None else [g + t for g, t in zip(group, terms)]
            placed = moved(group, 1, (j - outer // 2) * inner, lane, count - 2)
            summed = placed if summed is None else [s + p for s, p in zip(summed, placed)]
        out_ref[e] = jnp.concatenate(summed, axis=1)


def chosen(values, index):
    if len(set(values)) == 1:
        return jnp.int32(values[0])
    return sum(jnp.where(index == i, jnp.int32(v), 0) for i, v in enumerate(values))


def banded(steps, origins, height, slots, psf_ref, shifts_ref):
    taps = psf_ref.shape[1]
    radius = taps // 2
    sources = len(origins)
    paired = 2 * height
    rows_all = sources * height
    order = len(steps)
    block = rows_all // order
    depth = sources * slots * paired
    epoch = lax.axis_index("epoch")
    mine = lax.axis_index("vel")
    out_at = lax.broadcasted_iota(jnp.int32, (2 * rows_all, 1), 0)
    step = out_at // (2 * block)
    out_member = (out_at // block) % 2
    out_block = jnp.zeros_like(step)
    for k in range(order):
        target = chosen(steps[k], epoch)
        out_block = jnp.where(step == k, target, out_block)
    out_row = out_block * block + out_at % block
    in_at = lax.broadcasted_iota(jnp.int32, (1, depth), 1)
    in_member = (in_at // height) % 2
    in_slot = (in_at // paired) % slots
    place = in_at // (paired * slots)
    in_source = jnp.zeros_like(place)
    for s, row in enumerate(origins):
        in_source = jnp.where(place == s, chosen(row, mine), in_source)
    in_row = in_source * height + in_at % height
    shift_row = jnp.zeros_like(in_at)
    for e in range(slots):
        shift_row = jnp.where(in_slot == e, shifts_ref[1, epoch * slots + e], shift_row)
    target = out_row + shift_row
    tap = in_row - target + radius
    matrix = jnp.zeros((2 * rows_all, depth), jnp.float32)
    for k in range(taps):
        weight = jnp.zeros(in_at.shape, jnp.float32)
        for e in range(slots):
            weight = jnp.where(in_slot == e, psf_ref[e, k], weight)
        weight = jnp.where(in_member == 0, weight, weight * weight)
        matrix = jnp.where(tap == k, weight, matrix)
    keep = (target >= 0) & (target < rows_all) & (in_member == out_member)
    return jnp.where(keep, matrix, 0.0)


def split(x):
    high = x.astype(jnp.bfloat16)
    return high, (x - high.astype(jnp.float32)).astype(jnp.bfloat16)


def shifted(x, shift):
    tiles = tiles_of(x)
    lane = lax.broadcasted_iota(jnp.int32, tiles[0].shape, 1)
    turned = [pltpu.roll(t, lax.rem(LANES - shift, LANES), 1) for t in tiles]
    zero = jnp.zeros_like(turned[0])
    inside = (lane + shift >= 0) & (lane + shift < LANES)
    ahead = jnp.broadcast_to(shift, lane.shape) >= 0
    made = []
    for before, t, after in zip([zero] + turned[:-1], turned, turned[1:] + [zero]):
        made.append(jnp.where(inside, t, jnp.where(ahead, after, before)))
    return jnp.concatenate(made, axis=1)


def parts_of(matrix):
    high, low = split(matrix)
    return jnp.concatenate([high, high, low], axis=1)


def product_of(parts, pieces, shifts):
    images = [shifted(p[s, e], shift) for p in pieces for s in range(p.shape[0]) for e, shift in enumerate(shifts)]
    high, low = split(jnp.concatenate(images, axis=0))
    return jnp.dot(parts, jnp.concatenate([high, low, high], axis=0), preferred_element_type=jnp.float32)


def store_blocks(product, outs):
    at = 0
    for out in outs:
        rows = out.shape[-2]
        for m in range(out.shape[0]):
            out[m] = product[at : at + rows]
            at += rows


def matrix_kernel(steps, origins, height, psf_ref, shifts_ref, column_ref, *parts_refs):
    slots = column_ref.shape[0]
    matrix = banded(steps, origins, height, slots, psf_ref, shifts_ref)
    at = 0
    for ref in parts_refs:
        depth = ref.shape[1] // 3
        ref[...] = parts_of(matrix[:, at : at + depth])
        at += depth
    epoch = lax.axis_index("epoch")
    for e in range(slots):
        shift = shifts_ref[0, epoch * slots + e]
        column_ref[e] = jnp.full(column_ref.shape[1:], shift, jnp.int32)


def stack_kernel(count, added, column_ref, parts_ref, *refs):
    pieces, refs = refs[:count], refs[count:]
    shifts = [column_ref[e][0, 0] for e in range(column_ref.shape[0])]
    product = product_of(parts_ref[...], pieces, shifts)
    if added:
        product, refs = refs[0][...] + product, refs[1:]
    if len(refs) == 1:
        refs[0][...] = product
    else:
        store_blocks(product, refs)


def whole_kernel(steps, origins, psf_ref, shifts_ref, pieces_ref, *outs):
    slots, paired = pieces_ref.shape[1:3]
    parts = parts_of(banded(steps, origins, paired // 2, slots, psf_ref, shifts_ref))
    epoch = lax.axis_index("epoch")
    shifts = [shifts_ref[0, epoch * slots + e] for e in range(slots)]
    store_blocks(product_of(parts, [pieces_ref], shifts), outs)


def grant(bytes_used):
    return pltpu.CompilerParams(vmem_limit_bytes=min(4 * bytes_used, 60 << 20))


def send(array, axis, targets):
    return lax.ppermute(array, axis, list(enumerate(targets)))


def hand(array, targets, grid):
    pairs = []
    for i, t in enumerate(targets):
        for v in range(grid):
            pairs.append((i * grid + v, t * grid + (v ^ 1 if t == i else v)))
    return lax.ppermute(array, ("epoch", "vel"), pairs)


def per_device(science, variance, psf, shifts):
    slots, height, breadth = science.shape
    order = lax.axis_size("epoch")
    sources = lax.axis_size("vel")
    steps = STEPS
    if order != len(STEPS):
        steps = [[(i + k) % order for i in range(order)] for k in range(order)]
    paired = 2 * height
    shifts = shifts.reshape(shifts.shape[:2])
    filtered = pl.pallas_call(
        columns_kernel,
        out_shape=jax.ShapeDtypeStruct((slots, paired, breadth), jnp.float32),
        in_specs=[HBM, HBM, HBM],
        out_specs=VMEM,
        scratch_shapes=[
            pltpu.VMEM(science.shape, jnp.float32),
            pltpu.VMEM(science.shape, jnp.float32),
            pltpu.SMEM(psf.shape, jnp.float32),
            pltpu.SemaphoreType.DMA((3,)),
        ],
        compiler_params=grant(16 * science.size),
        name="columns",
    )(*(pltpu.with_memory_space_constraint(a, pltpu.HBM) for a in (science, variance, psf)))
    rows_all = sources * height
    block = rows_all // order
    depth = sources * slots * paired
    used = grant(4 * (sources * filtered.size + 2 * rows_all * (depth + breadth)))
    chunk = jax.ShapeDtypeStruct((2, block, breadth), jnp.float32)
    if sources == 2 * len(ROUNDS[0]):
        rounds = [[2 * t + c for t in targets for c in range(2)] for targets in ROUNDS]
        arrived = [send(filtered, "vel", targets) for targets in rounds]
        own = jnp.stack([filtered] + arrived[:-1])
        last = arrived[-1][None]
        sibling = [v ^ 1 for v in range(sources)]
        twin = send(own, "vel", sibling)
        twin_last = send(last, "vel", sibling)
        origins = [list(range(sources))] + [[t.index(v) for v in range(sources)] for t in rounds]
        origins = origins + [[row[v ^ 1] for v in range(sources)] for row in origins]
        groups = [[own, last], [twin, twin_last]]
        depths = [sum(p.shape[0] for p in g) * slots * paired for g in groups]
        column, *parts = pl.pallas_call(
            functools.partial(matrix_kernel, steps, origins, height),
            out_shape=[jax.ShapeDtypeStruct((slots, 8, LANES), jnp.int32)]
            + [jax.ShapeDtypeStruct((2 * rows_all, 3 * d), jnp.bfloat16) for d in depths],
            in_specs=[SMEM] * 2,
            out_specs=[VMEM] * (1 + len(depths)),
            compiler_params=used,
            name="matrix",
        )(psf, shifts)
        partial = []
        for name, group, left in zip(("early", "late"), groups, parts):
            shapes = [jax.ShapeDtypeStruct((2 * rows_all, breadth), jnp.float32)]
            if name == "late":
                shapes = [chunk] * order
            operands = [column, left, *group, *partial]
            partial = pl.pallas_call(
                functools.partial(stack_kernel, len(group), bool(partial)),
                out_shape=shapes,
                in_specs=[VMEM] * len(operands),
                out_specs=[VMEM] * len(shapes),
                compiler_params=used,
            )(*operands)
        chunks = partial
    else:
        chunks = pl.pallas_call(
            functools.partial(whole_kernel, steps, [[s] * sources for s in range(sources)]),
            out_shape=[chunk] * order,
            in_specs=[SMEM] * 2 + [VMEM],
            out_specs=[VMEM] * order,
            compiler_params=used,
            name="stack",
        )(psf, shifts, lax.all_gather(filtered, "vel"))
    terms = []
    for k, targets in enumerate(steps):
        came = hand(chunks[k], targets, sources)
        kept = chosen([int(t == i) for i, t in enumerate(targets)], lax.axis_index("epoch"))
        terms.append(jnp.where(kept == 1, chunks[k], came))
    psi, phi = (sum(t[m] for t in terms) for m in range(2))
    return (psi / jnp.sqrt(phi))[None]


def solution(mesh):
    return jax.shard_map(
        per_device,
        mesh=mesh,
        in_specs=(
            P("epoch", "vel", None),
            P("epoch", "vel", None),
            P("epoch", None),
            P(None, None, "vel"),
        ),
        out_specs=P("vel", "epoch", None),
        check_vma=False,
    )
```
